512 devices in a mesh: grp: 8 (over y_hi, core), ctx: 64 (over x, y_lo, z).
Axes of the slice: x: 4, y: 8 (y_hi: 4, y_lo: 2; y = y_hi * 2 + y_lo), z: 8, core: 2. Of those that a mesh axis runs over, the one named last changes fastest.
Arguments:
- queries: bfloat16 [65536, 4096], P(('grp', 'ctx')), may hold values from -6 to 6
- keys: bfloat16 [65536, 512], P(('grp', 'ctx')), may hold values from -6 to 6
- values: bfloat16 [65536, 512], P(('grp', 'ctx')), may hold values from -6 to 6
- d_unit: bfloat16 [65536, 4096], P(('grp', 'ctx')), may hold values from -6 to 6
- token_terms: float32 [65536], P(('grp', 'ctx')), may hold values from -4 to 4
- spans: int32 [128, 3], P('grp'), may hold values from 1 to 3, as said below
Outputs:
- attended: bfloat16 [65536, 4096], P(('grp', 'ctx'))
- query_grad: bfloat16 [65536, 4096], P(('grp', 'ctx'))
- key_gradient: bfloat16 [65536, 512], P(('grp', 'ctx'))
- value_gradient: bfloat16 [65536, 512], P(('grp', 'ctx'))
The draws below stay inside these ranges and needn't reach their ends.
Inputs may be any that keep to these rules, and one draw needn't show every extreme that they name: `spans`: each row's 16 examples have 3 to 5 tiles each and fill its 64 tiles exactly; every span has at least one tile; every row has an example of exactly 5 tiles.
All inputs are finite; a program needn't handle non-finite values.
Results may differ from the reference program's by a relative error of at most 0.012.
The reference program's roundings to bfloat16 on the way count: a program that leaves them out, or rounds other values in their place, can miss the bound.
Values may be sent and summed in bfloat16 or wider, within the bound.
No kernel may reach another device: no remote copies, remote signals or barrier semaphores. Data moves between devices by JAX's collectives and lax.ppermute only.
A program may use at most 128 MiB of HBM per device.

```python
import jax
import jax.numpy as jnp
from jax import lax

QUERY_HEADS = 32
KEY_VALUE_HEADS = 4
HEAD_SIZE = 128
TILE_TOKENS = 128
BASE = 4
MAX_TILES = 5
EX = 16
TOTAL_TOKENS = 65536
N_GRP = 8
N_CTX = 64


def draw_queries(key, part):
    row_count = N_GRP * N_CTX * TILE_TOKENS
    final_output = jax.random.truncated_normal(jax.random.fold_in(key, 11), -4.0, 4.0, (row_count, QUERY_HEADS * HEAD_SIZE), jnp.float32)
    return final_output.astype(jnp.bfloat16)


def draw_keys(key, part):
    row_count = N_GRP * N_CTX * TILE_TOKENS
    final_output = jax.random.truncated_normal(jax.random.fold_in(key, 12), -4.0, 4.0, (row_count, KEY_VALUE_HEADS * HEAD_SIZE), jnp.float32)
    return final_output.astype(jnp.bfloat16)


def draw_spans(key, part):
    pair_count = EX // 2
    surplus = jax.random.randint(jax.random.fold_in(key, 41), (N_GRP, pair_count), -1, 2)
    signs_first = 2 * jax.random.randint(jax.random.fold_in(key, 42), (N_GRP, 1), 0, 2) - 1
    leading = jnp.arange(pair_count)[None, :] == 0
    surplus = jnp.where(leading, signs_first, surplus)
    counts = jnp.concatenate([BASE + surplus, BASE - surplus], axis=1).astype(jnp.int32)
    order_keys = jax.random.randint(jax.random.fold_in(key, 43), (N_GRP, EX), 0, 1 << 20) * EX + jnp.arange(EX)[None, :]
    ordering = jnp.argsort(order_keys, axis=1)
    counts = jnp.take_along_axis(counts, ordering, axis=1)
    extra_prompt = jax.random.randint(jax.random.fold_in(key, 44), (N_GRP, EX), 0, counts - 2)
    extra_chosen = jax.random.randint(jax.random.fold_in(key, 45), (N_GRP, EX), 0, counts - 2 - extra_prompt)
    prompt = 1 + extra_prompt
    chosen = 1 + extra_chosen
    rejected = counts - prompt - chosen
    return jnp.stack([prompt, chosen, rejected], axis=-1).reshape(N_GRP * EX, 3).astype(jnp.int32)


def levels(stream_key, shape, cuts, low, largest):
    def one(dim, parts):
        steps = jax.random.uniform(jax.random.fold_in(jax.random.fold_in(stream_key, 6), dim), (parts,), jnp.float32, low / len(cuts), largest / len(cuts))
        return jnp.repeat(jnp.exp(steps), shape[dim] // parts).reshape((-1,) + (1,) * (len(shape) - dim - 1))

    gain = one(*cuts[0])
    for cut in cuts[1:]:
        gain = gain * one(*cut)
    return gain


def noise(key, shape, width, most, cuts=(), kind=jnp.bfloat16):
    drawn = jax.random.normal(key, shape, jnp.float32) * width
    if len(cuts) > 0:
        drawn = levels(key, shape, cuts, -0.22, 0.18) * drawn
    return jnp.clip(drawn, min=-most, max=most).astype(kind)


def setup_inputs(seed: int = 0) -> dict:
    key_list = jax.random.split(jax.random.key(seed), 7)
    return {
        "queries": draw_queries(jax.random.fold_in(key_list[6], 71), 0),
        "keys": draw_keys(jax.random.fold_in(key_list[6], 71), 0),
        "values": noise(key_list[2], (TOTAL_TOKENS, KEY_VALUE_HEADS * HEAD_SIZE), 1.0, 6.0, ((0, 512),)),
        "d_unit": noise(key_list[3], (TOTAL_TOKENS, QUERY_HEADS * HEAD_SIZE), 1.0, 6.0, ((0, 512),)),
        "token_terms": noise(key_list[4], (TOTAL_TOKENS,), 0.5, 4.0, ((0, 512),), jnp.float32),
        "spans": draw_spans(jax.random.fold_in(key_list[6], 71), 0),
    }


preference_beta = 0.3


def tile_meta(spans_row, tile_index):
    counts = spans_row[:, 0] + spans_row[:, 1] + spans_row[:, 2]
    ends = jnp.cumsum(counts).astype(jnp.int32)
    starts = ends - counts
    example = jnp.sum((starts[None, :] <= tile_index[:, None]).astype(jnp.int32), axis=1) - 1
    labels = jnp.arange(spans_row.shape[0], dtype=jnp.int32)
    hits = (example[:, None] == labels[None, :]).astype(jnp.int32)
    within = tile_index - jnp.sum(hits * starts[None, :], axis=1)
    prompt = jnp.sum(hits * spans_row[None, :, 0], axis=1)
    chosen = jnp.sum(hits * spans_row[None, :, 1], axis=1)
    kind = jnp.where(within < prompt, 0, jnp.where(within < prompt + chosen, 1, 2)).astype(jnp.int32)
    return example, kind, hits


def live_tiles(spans_row, position):
    key_tiles = position - jnp.arange(MAX_TILES, dtype=jnp.int32)
    key_example, key_kind, unused_hits = tile_meta(spans_row, key_tiles)
    own_example, own_kind, own_hits = tile_meta(spans_row, jnp.reshape(position, (1,)).astype(jnp.int32))
    blocked = (own_kind[0] == 2) & (key_kind == 1)
    return (key_tiles >= 0) & (key_example == own_example[0]) & jnp.logical_not(blocked)


def tile_grads(query_tile_block, key_pad, value_pad, gradient_tile, spans_row, position):
    heads_per_group = QUERY_HEADS // KEY_VALUE_HEADS
    score_scale = HEAD_SIZE ** -0.5
    key_span_window = lax.dynamic_slice_in_dim(key_pad, position, MAX_TILES, 0)[::-1]
    value_span_window = lax.dynamic_slice_in_dim(value_pad, position, MAX_TILES, 0)[::-1]
    query_heads = query_tile_block.astype(jnp.float32).reshape(TILE_TOKENS, KEY_VALUE_HEADS, heads_per_group, HEAD_SIZE)
    key_heads = key_span_window.astype(jnp.float32).reshape(MAX_TILES, TILE_TOKENS, KEY_VALUE_HEADS, HEAD_SIZE)
    value_heads = value_span_window.astype(jnp.float32).reshape(MAX_TILES, TILE_TOKENS, KEY_VALUE_HEADS, HEAD_SIZE)
    group_heads = gradient_tile.astype(jnp.float32).reshape(TILE_TOKENS, KEY_VALUE_HEADS, heads_per_group, HEAD_SIZE)
    scores = jnp.einsum("ihgc,djhc->dhgij", query_heads, key_heads) * score_scale
    live = live_tiles(spans_row, position)
    causal = jnp.arange(TILE_TOKENS)[:, None] >= jnp.arange(TILE_TOKENS)[None, :]
    later = (jnp.arange(MAX_TILES) > 0)[:, None, None]
    allowed = live[:, None, None] & (later | causal[None, :, :])
    scores = jnp.where(allowed[:, None, None, :, :], scores, -jnp.inf)
    row_max = jnp.max(scores, axis=(0, 4), keepdims=True)
    lse = row_max + jnp.log(jnp.sum(jnp.exp(scores - row_max), axis=(0, 4), keepdims=True))
    probability = jnp.exp(scores - lse)
    rounded = lax.optimization_barrier(probability.astype(jnp.bfloat16)).astype(jnp.float32)
    output_sum = jnp.einsum("dhgij,djhc->ihgc", rounded, value_heads)
    row_dots = jnp.transpose(jnp.sum(group_heads * output_sum, axis=-1), (1, 2, 0))[None, :, :, :, None]
    dprob = jnp.einsum("ihgc,djhc->dhgij", group_heads, value_heads)
    dscores = probability * (dprob - row_dots) * score_scale
    dscores = lax.optimization_barrier(dscores.astype(jnp.bfloat16)).astype(jnp.float32)
    query_part = jnp.einsum("dhgij,djhc->ihgc", dscores, key_heads)
    key_portion = jnp.einsum("dhgij,ihgc->djhc", dscores, query_heads)
    value_portion = jnp.einsum("dhgij,ihgc->djhc", rounded, group_heads)
    return (output_sum.astype(jnp.bfloat16).reshape(TILE_TOKENS, QUERY_HEADS * HEAD_SIZE),
            query_part.astype(jnp.bfloat16).reshape(TILE_TOKENS, QUERY_HEADS * HEAD_SIZE),
            key_portion.reshape(MAX_TILES, TILE_TOKENS, KEY_VALUE_HEADS * HEAD_SIZE),
            value_portion.reshape(MAX_TILES, TILE_TOKENS, KEY_VALUE_HEADS * HEAD_SIZE))


def row_grads(query_row, key_row, value_row, cotangent_row, spans_row):
    key_pad = jnp.pad(key_row, ((MAX_TILES - 1, 0), (0, 0), (0, 0)))
    value_pad = jnp.pad(value_row, ((MAX_TILES - 1, 0), (0, 0), (0, 0)))

    def one_tile(position):
        return tile_grads(query_row[position], key_pad, value_pad, cotangent_row[position], spans_row, position)

    attended, query_grad, key_parts, value_parts = lax.map(one_tile, jnp.arange(N_CTX, dtype=jnp.int32))
    key_parts = jnp.pad(key_parts, ((0, MAX_TILES - 1), (0, 0), (0, 0), (0, 0)))
    value_parts = jnp.pad(value_parts, ((0, MAX_TILES - 1), (0, 0), (0, 0), (0, 0)))
    key_gradient = jnp.zeros((N_CTX, TILE_TOKENS, KEY_VALUE_HEADS * HEAD_SIZE), jnp.float32)
    value_gradient = jnp.zeros((N_CTX, TILE_TOKENS, KEY_VALUE_HEADS * HEAD_SIZE), jnp.float32)
    for start_shift in range(MAX_TILES):
        key_gradient = key_gradient + key_parts[start_shift:start_shift + N_CTX, start_shift]
        value_gradient = value_gradient + value_parts[start_shift:start_shift + N_CTX, start_shift]
    return attended, query_grad, key_gradient.astype(jnp.bfloat16), value_gradient.astype(jnp.bfloat16)


def reference(queries, keys, values, d_unit, token_terms, spans):
    row_spans = spans.reshape(N_GRP, EX, 3)
    tile_ids = jnp.arange(N_CTX, dtype=jnp.int32)
    metas = jax.vmap(lambda spans_row: tile_meta(spans_row, tile_ids))(row_spans)
    tile_kind = metas[1]
    tile_hits = metas[2].astype(jnp.float32)
    tile_sums = jnp.sum(token_terms.reshape(N_GRP, N_CTX, TILE_TOKENS), axis=-1)
    polarity = jnp.where(tile_kind == 1, 1.0, jnp.where(tile_kind == 2, -1.0, 0.0)).astype(jnp.float32)
    margins = jnp.sum(tile_hits * (polarity * tile_sums)[:, :, None], axis=1)
    center = jnp.sum(margins) / (N_GRP * EX)
    weights = jax.nn.sigmoid(preference_beta * (center - margins))
    tile_weight = jnp.sum(tile_hits * weights[:, None, :], axis=-1)
    unit_rows = d_unit.reshape(N_GRP, N_CTX, TILE_TOKENS, QUERY_HEADS * HEAD_SIZE).astype(jnp.float32)
    output_gradient = (tile_weight[:, :, None, None] * unit_rows).astype(jnp.bfloat16)
    query_rows = queries.reshape(N_GRP, N_CTX, TILE_TOKENS, QUERY_HEADS * HEAD_SIZE)
    key_row_block = keys.reshape(N_GRP, N_CTX, TILE_TOKENS, KEY_VALUE_HEADS * HEAD_SIZE)
    value_row_block = values.reshape(N_GRP, N_CTX, TILE_TOKENS, KEY_VALUE_HEADS * HEAD_SIZE)
    output_list = lax.map(lambda items: row_grads(items[0], items[1], items[2], items[3], items[4]),
                      (query_rows, key_row_block, value_row_block, output_gradient, row_spans))
    attended = output_list[0].reshape(TOTAL_TOKENS, QUERY_HEADS * HEAD_SIZE)
    query_grad = output_list[1].reshape(TOTAL_TOKENS, QUERY_HEADS * HEAD_SIZE)
    key_gradient = output_list[2].reshape(TOTAL_TOKENS, KEY_VALUE_HEADS * HEAD_SIZE)
    value_gradient = output_list[3].reshape(TOTAL_TOKENS, KEY_VALUE_HEADS * HEAD_SIZE)
    return (attended, query_grad, key_gradient, value_gradient)
```

```python
import jax
import jax.numpy as jnp
from jax import lax
from jax.experimental import pallas as pl
from jax.experimental.pallas import tpu as pltpu
from jax.sharding import PartitionSpec as P

QUERY_HEADS = 32
KEY_VALUE_HEADS = 4
GROUP = QUERY_HEADS // KEY_VALUE_HEADS
HEAD_SIZE = 128
TILE = 128
MAX_TILES = 5
EXAMPLES = 16
LOW = -1e30
SCALE = HEAD_SIZE ** (-0.5)

preference_beta = 0.3


def copy_for_each(shard, axis):
    copies = jnp.broadcast_to(shard, (lax.axis_size(axis), *shard.shape))
    return lax.all_to_all(copies, axis, split_axis=0, concat_axis=0, tiled=True)


def from_behind(shard, axis, by):
    length = lax.axis_size(axis)
    pairs = [(i, i + by) for i in range(length) if 0 <= i + by < length]
    return lax.ppermute(shard, axis, pairs)


def own_place(spans, position):
    counts = spans[:, 0] + spans[:, 1] + spans[:, 2]
    ends = jnp.cumsum(counts)
    starts = ends - counts
    mine = ((starts <= position) & (position < ends)).astype(jnp.int32)
    start = jnp.sum(mine * starts)
    prompt_end = start + jnp.sum(mine * spans[:, 0])
    chosen_end = prompt_end + jnp.sum(mine * spans[:, 1])
    end = start + jnp.sum(mine * counts)
    return start, prompt_end, chosen_end, end


def own_weight(token_terms, start, prompt_end, chosen_end, end, position):
    polarity = jnp.where(
        position < prompt_end, 0.0, jnp.where(position < chosen_end, 1.0, -1.0)
    ).astype(jnp.float32)
    own_margin = polarity * jnp.sum(token_terms)
    row_margins = copy_for_each(own_margin[None], "ctx")[:, 0]
    tiles = jnp.arange(row_margins.shape[0], dtype=jnp.int32)
    inside = (tiles >= start) & (tiles < end)
    margin = jnp.sum(jnp.where(inside, row_margins, 0.0))
    total = jnp.sum(copy_for_each(jnp.sum(row_margins)[None], "grp"))
    center = total / (EXAMPLES * lax.axis_size("grp"))
    return jax.nn.sigmoid(preference_beta * (center - margin))


def dot(a, b, dims):
    return lax.dot_general(a, b, (dims, ((), ())), preferred_element_type=jnp.float32)


def attention_kernel(live_ref, weight_ref, q_ref, d_ref, *refs):
    k_refs, v_refs = refs[0:5], refs[5:10]
    att_ref, dq_ref = refs[10:12]
    dk_refs, dv_refs = refs[12:17], refs[17:22]
    q_scr, c_scr, s_scr, p_scr, m_scr, l_scr, r_scr, o_scr, g_scr = refs[22:]
    weight = weight_ref[0]
    for h in range(GROUP):
        cols = slice(h * HEAD_SIZE, (h + 1) * HEAD_SIZE)
        rows = slice(h * TILE, (h + 1) * TILE)
        q_scr[rows, :] = q_ref[:, cols]
        c_scr[rows, :] = (weight * d_ref[:, cols].astype(jnp.float32)).astype(jnp.bfloat16)

    def scores(s):
        raw = dot(k_refs[s][...], q_scr[...], ((1,), (1,))) * SCALE
        if s == 0:
            key_at = lax.broadcasted_iota(jnp.int32, raw.shape, 0)
            query_at = lax.broadcasted_iota(jnp.int32, raw.shape, 1) % TILE
            raw = jnp.where(key_at <= query_at, raw, LOW)
        s_scr[s] = raw
        top = jnp.max(raw, axis=0, keepdims=True)
        m_scr[...] = top if s == 0 else jnp.maximum(m_scr[...], top)

    def weights(s):
        grown = jnp.exp(s_scr[s] - m_scr[...])
        s_scr[s] = grown
        total = jnp.sum(grown, axis=0, keepdims=True)
        l_scr[...] = total if s == 0 else l_scr[...] + total

    def outputs(s):
        probability = s_scr[s] * l_scr[...]
        rounded = probability.astype(jnp.bfloat16)
        s_scr[s] = probability
        p = dot(v_refs[s][...], c_scr[...], ((1,), (1,)))
        p_scr[s] = p
        dots = jnp.sum(rounded.astype(jnp.float32) * p, axis=0, keepdims=True)
        r_scr[...] = dots if s == 0 else r_scr[...] + dots
        dv_refs[s][...] = dot(rounded, c_scr[...], ((1,), (0,))).astype(dv_refs[s].dtype)
        part = dot(v_refs[s][...].T, rounded, ((1,), (0,)))
        o_scr[...] = part if s == 0 else o_scr[...] + part

    def gradients(s):
        ds = (s_scr[s] * (p_scr[s] - r_scr[...]) * SCALE).astype(jnp.bfloat16)
        dk_refs[s][...] = dot(ds, q_scr[...], ((1,), (0,))).astype(dk_refs[s].dtype)
        part = dot(k_refs[s][...].T, ds, ((1,), (0,)))
        g_scr[...] = part if s == 0 else g_scr[...] + part

    def each(step):
        step(0)
        for s in range(1, MAX_TILES):
            pl.when(live_ref[s] != 0)(lambda s=s: step(s))

    each(scores)
    each(weights)
    l_scr[...] = 1.0 / l_scr[...]
    each(outputs)
    each(gradients)
    for s in range(1, MAX_TILES):

        @pl.when(live_ref[s] == 0)
        def _():
            dk_refs[s][...] = jnp.zeros_like(dk_refs[s])
            dv_refs[s][...] = jnp.zeros_like(dv_refs[s])

    for h in range(GROUP):
        cols = slice(h * HEAD_SIZE, (h + 1) * HEAD_SIZE)
        rows = slice(h * TILE, (h + 1) * TILE)
        att_ref[:, cols] = o_scr[:, rows].T.astype(jnp.bfloat16)
        dq_ref[:, cols] = g_scr[:, rows].T.astype(jnp.bfloat16)


def attention(live, weight, queries, d_unit, keys, values):
    wide = pl.BlockSpec((TILE, GROUP * HEAD_SIZE), lambda g: (0, g))
    narrow = pl.BlockSpec((TILE, HEAD_SIZE), lambda g: (0, g))
    scalars = pl.BlockSpec(memory_space=pltpu.SMEM)
    lanes = GROUP * TILE
    big = jax.ShapeDtypeStruct(queries.shape, jnp.bfloat16)
    kinds = [jnp.float32] * 4 + [jnp.bfloat16]
    parts = [jax.ShapeDtypeStruct((TILE, KEY_VALUE_HEADS * HEAD_SIZE), kind) for kind in kinds]
    out = pl.pallas_call(
        attention_kernel,
        grid=(KEY_VALUE_HEADS,),
        in_specs=[scalars, scalars, wide, wide] + [narrow] * 10,
        out_specs=[wide, wide] + [narrow] * 10,
        out_shape=[big, big] + parts + parts,
        scratch_shapes=[
            pltpu.VMEM((lanes, HEAD_SIZE), jnp.bfloat16),
            pltpu.VMEM((lanes, HEAD_SIZE), jnp.bfloat16),
            pltpu.VMEM((MAX_TILES, TILE, lanes), jnp.float32),
            pltpu.VMEM((MAX_TILES, TILE, lanes), jnp.float32),
            pltpu.VMEM((1, lanes), jnp.float32),
            pltpu.VMEM((1, lanes), jnp.float32),
            pltpu.VMEM((1, lanes), jnp.float32),
            pltpu.VMEM((HEAD_SIZE, lanes), jnp.float32),
            pltpu.VMEM((HEAD_SIZE, lanes), jnp.float32),
        ],
        cost_estimate=pl.CostEstimate(flops=4_000_000_000, bytes_accessed=8_000_000, transcendentals=2_600_000),
        name="attention",
    )(live, weight, queries, d_unit, *keys, *values)
    return out[0], out[1], out[2:7], out[7:12]


def per_device(queries, keys, values, d_unit, token_terms, spans):
    position = lax.axis_index("ctx")
    key_tiles, value_tiles = [keys], [values]
    for _ in range(1, MAX_TILES):
        key_tiles.append(from_behind(key_tiles[-1], "ctx", 1))
        value_tiles.append(from_behind(value_tiles[-1], "ctx", 1))
    start, prompt_end, chosen_end, end = own_place(spans, position)
    weight = own_weight(token_terms, start, prompt_end, chosen_end, end, position)
    tiles = position - jnp.arange(MAX_TILES, dtype=jnp.int32)
    chosen = (tiles >= prompt_end) & (tiles < chosen_end)
    blocked = (position >= chosen_end) & chosen
    live = ((tiles >= start) & jnp.logical_not(blocked)).astype(jnp.int32)
    attended, query_grad, key_parts, value_parts = attention(
        live, weight[None], queries, d_unit, key_tiles, value_tiles
    )
    key_sum, value_sum = key_parts[-1], value_parts[-1]
    for shift in range(MAX_TILES - 2, -1, -1):
        key_sum = from_behind(key_sum, "ctx", -1).astype(jnp.float32) + key_parts[shift]
        value_sum = from_behind(value_sum, "ctx", -1).astype(jnp.float32) + value_parts[shift]
        key_sum, value_sum = key_sum.astype(jnp.bfloat16), value_sum.astype(jnp.bfloat16)
    return attended, query_grad, key_sum, value_sum


def solution(mesh):
    return jax.shard_map(
        per_device,
        mesh=mesh,
        in_specs=(
            P(("grp", "ctx"), None),
            P(("grp", "ctx"), None),
            P(("grp", "ctx"), None),
            P(("grp", "ctx"), None),
            P(("grp", "ctx")),
            P("grp", None),
        ),
        out_specs=(
            P(("grp", "ctx"), None),
            P(("grp", "ctx"), None),
            P(("grp", "ctx"), None),
            P(("grp", "ctx"), None),
        ),
        check_vma=False,
    )
```
